256 devices in a mesh: seq: 16 (over z, x_lo), head: 4 (over x_hi, core), req: 4 (over y).
Axes of the slice: x: 4 (x_hi: 2, x_lo: 2; x = x_hi * 2 + x_lo), y: 4, z: 8, core: 2. Of those that a mesh axis runs over, the one named last changes fastest.
Arguments:
- queries: bfloat16 [32768, 2560], P(('req', 'seq'), 'head'), parts along dimension 0, may hold values from -8 to 8
- keys: bfloat16 [32768, 2560], P(('req', 'seq'), 'head'), parts along dimension 0, may hold values from -8 to 8
- values: bfloat16 [32768, 2560], P(('req', 'seq'), 'head'), parts along dimension 0, may hold values from -8 to 8
- clip_ids: int32 [32768], P('req'), parts along dimension 0, may hold values from 0 to 3, never falling along the last dimension, each value on 1 to 3072 neighbouring positions
- plan: int32 [256], P('req'), parts along dimension 0, may hold values from 0 to 15, as said below
Outputs:
- attended: bfloat16 [32768, 2560], P(('req', 'seq'), 'head'), parts along dimension 0
- log_normalizer: float32 [20, 32768], P('head', ('req', 'seq')), parts along dimension 1
The draws below stay inside these ranges and needn't reach their ends.
There are 4 independent parts, one for each index of `req`. The reference program is written for one: setup_inputs(seed, part) draws one part's arguments, and reference() takes and returns one part's arrays. A program takes and returns all parts, laid end to end along the dimension named above; each array names one. Nothing has to cross between parts.
Inputs may be any that keep to these rules, and one draw needn't show every extreme that they name: `plan`: every index along seq computes exactly 4 blocks, and of the 4 blocks held by one index of seq (blocks k * 4 to k * 4 + 3 on index k) at most 1 go to the same index; some pair of indices reaches 1. `clip_ids`: clip ids never fall along the tokens; each clip holds 1 to 3072 tokens and one holds exactly 3072.
All inputs are finite; a program needn't handle non-finite values.
Results may differ from the reference program's by a relative error of at most 0.007.
Values may be sent and summed in bfloat16 or wider, within the bound.
A program may use at most 128 MiB of HBM per device.

```python
import math
import jax
import jax.numpy as jnp
import numpy as np
from jax import lax

HEADS = 20
HD = 128
BLOCK = 128
CLIPS = 4
GROUP = 16
TOKENS = 8192
BLK_DEV = 4
BLOCKS = 64
CAP = 1
LONGEST = 3072


def draw_queries(key, part):
    drawn = jnp.clip(jax.random.normal(jax.random.fold_in(key, 1), (TOKENS, HEADS * HD), jnp.float32), -6.0, 6.0)
    return jnp.clip(drawn, -8.0, 8.0).astype(jnp.bfloat16)


def draw_keys(key, part):
    drawn = jnp.clip(jax.random.normal(jax.random.fold_in(key, 2), (TOKENS, HEADS * HD), jnp.float32), -6.0, 6.0)
    return jnp.clip(drawn, -8.0, 8.0).astype(jnp.bfloat16)


def draw_values(key, part):
    drawn = jnp.clip(jax.random.normal(jax.random.fold_in(key, 5), (TOKENS, HEADS * HD), jnp.float32), -6.0, 6.0)
    return jnp.clip(drawn, -8.0, 8.0).astype(jnp.bfloat16)


def draw_plan(key, part):
    key_sigma, key_tau, key_offset, key_order = jax.random.split(jax.random.fold_in(key, 11), 4)
    sigma = jax.random.permutation(key_sigma, GROUP)
    tau = jax.random.permutation(key_tau, GROUP)
    offsets = jax.random.permutation(key_offset, GROUP * CAP)[:BLK_DEV] // CAP
    scores_int = jax.random.randint(key_order, (GROUP, BLK_DEV), 0, 1 << 20) * BLK_DEV + jnp.arange(BLK_DEV)[None, :]
    within = jnp.argsort(scores_int, axis=1)
    shifted = (sigma[:, None] + offsets[within]) % GROUP
    return tau[shifted].reshape(BLOCKS).astype(jnp.int32)


def profile(amount, total, bound, lean):
    portions = [(1 << 20) // math.isqrt(grade ** lean) + 1 for grade in range(2, amount + 1)]
    spare, counts = total - bound - (amount - 1), [1] * (amount - 1)
    while spare > 0:
        candidates = [i for i in range(amount - 1) if counts[i] < bound]
        whole, remaining = sum([portions[i] for i in candidates]), spare
        for i in candidates:
            addition = min(bound - counts[i], max(1, remaining * portions[i] // whole), spare)
            counts[i] = counts[i] + addition
            spare = spare - addition
    return np.array([bound] + counts)


def ragged(key, amount, total, reach, slope):
    if amount == 2:
        one = jax.random.randint(key, (), max(1, total - reach), min(reach, total - 1) + 1)
        return jnp.stack([one, total - one])
    sizes = jnp.asarray(profile(amount, total, reach, slope), jnp.int32)
    pairs = (amount - 1) // 2
    giver, receiver = sizes[1:1 + 2 * pairs:2], sizes[2:2 + 2 * pairs:2]
    margin = jnp.minimum(giver - 1, reach - receiver)
    moved = jax.random.randint(jax.random.fold_in(key, 1), (pairs,), 0, 1 << 20) % (margin + 1)
    sizes = sizes.at[1:1 + 2 * pairs:2].set(giver - moved).at[2:2 + 2 * pairs:2].set(receiver + moved)
    return sizes[jax.random.permutation(jax.random.fold_in(key, 2), amount)]


def setup_inputs(seed: int = 0, part: int = 0) -> dict:
    key_list = jax.random.split(jax.random.key(seed), 6)
    own_keys = jax.random.split(jax.random.fold_in(key_list[5], part), 6)
    queries = draw_queries(jax.random.fold_in(jax.random.fold_in(key_list[5], part), 71), part)
    keys = draw_keys(jax.random.fold_in(jax.random.fold_in(key_list[5], part), 71), part)
    values = draw_values(jax.random.fold_in(jax.random.fold_in(key_list[5], part), 71), part)
    clip_ids = jnp.searchsorted(jnp.cumsum(ragged(own_keys[3], CLIPS, TOKENS, LONGEST, 2)), jnp.arange(TOKENS), side="right").astype(jnp.int32)
    plan = draw_plan(jax.random.fold_in(jax.random.fold_in(key_list[5], part), 71), part)
    return {"queries": queries, "keys": keys, "values": values, "clip_ids": clip_ids, "plan": plan}


def reference(queries, keys, values, clip_ids, plan):
    score_scale = 1.0 / (HD ** 0.5)
    query_heads = jnp.transpose(queries.reshape(TOKENS, HEADS, HD), (1, 0, 2))
    key_heads = jnp.transpose(keys.reshape(TOKENS, HEADS, HD), (1, 0, 2))
    value_heads = jnp.transpose(values.reshape(TOKENS, HEADS, HD), (1, 0, 2))
    same_clip = clip_ids[:, None] == clip_ids[None, :]

    def one_head(operands):
        query_one, key_one, value_one = operands
        scores = jnp.dot(query_one, key_one.T, preferred_element_type=jnp.float32) * score_scale
        masked = jnp.where(same_clip, scores, jnp.float32(-1e30))
        row_max = jnp.max(masked, axis=1)
        exponent = jnp.where(same_clip, jnp.exp(masked - row_max[:, None]), jnp.float32(0.0))
        row_sum = jnp.sum(exponent, axis=1)
        mixed = jnp.dot(exponent.astype(jnp.bfloat16), value_one, preferred_element_type=jnp.float32) / row_sum[:, None]
        return mixed.astype(jnp.bfloat16), row_max + jnp.log(row_sum)

    mixed_all, log_total = lax.map(one_head, (query_heads, key_heads, value_heads))
    attended = jnp.transpose(mixed_all, (1, 0, 2)).reshape(TOKENS, HEADS * HD)
    block_index = jnp.arange(BLOCKS, dtype=jnp.int32)
    order_blocks = jnp.argsort(plan.astype(jnp.int32) * BLOCKS + block_index).astype(jnp.int32)
    token_order = (order_blocks[:, None] * BLOCK + jnp.arange(BLOCK, dtype=jnp.int32)[None, :]).reshape(-1)
    log_normalizer = log_total[:, token_order]
    return attended, log_normalizer
```

```python
import functools

import jax
import jax.numpy as jnp
from jax import lax
from jax.experimental import pallas as pl
from jax.experimental.pallas import tpu as pltpu
from jax.sharding import PartitionSpec as P

HD = 128
ROWS = 512
HALF = 256
NZ = 8
REACH = 6
APART = 32768.0
SCALE = 1.0 / HD**0.5
TO_EXP2 = 1.4426950408889634 * SCALE
MESH = pl.DeviceIdType.MESH


def kernel(
    q_in, k_in, v_in, ids_ref, plan_ref,
    att, lg_out,
    kv, qu, ou, kv5, q5, o5, mk, m_ref, acc_ref, lg, lg5, lg_all, lg5_all,
    q_send, k_send, v_send, x_send, c_send, f_send, ch_send, c5_send, o_send, o5_send, lg_send, lg5_send,
    q_recv, kv_recv, x_recv, c_recv, f_recv, chl_recv, chr_recv, c5_recv, o_recv, o5_recv, lg_recv, lg5_recv,
):
    seq = lax.axis_index("seq")
    head = lax.axis_index("head")
    z, x = seq // 2, seq % 2
    xh, c = head // 2, head % 2
    g, i_head = z % 2, z // 2
    kb5 = 2 * z + c

    def at(zz, xx, cc):
        return {"seq": 2 * zz + xx, "head": 2 * xh + cc}

    def remote(src, dst, send, recv, where):
        return pltpu.make_async_remote_copy(
            src_ref=src, dst_ref=dst, send_sem=send, recv_sem=recv, device_id=where, device_id_type=MESH
        )

    def arrived(dst, recv):
        remote(dst, dst, recv, recv, at(z, x, 1 - c)).wait_recv()

    barrier = pltpu.get_barrier_semaphore()

    def greet(t, carry):
        other_seq, other_c = t // 2, t % 2

        @pl.when(jnp.logical_or(other_seq != seq, other_c != c))
        def _():
            pl.semaphore_signal(
                barrier, inc=1, device_id={"seq": other_seq, "head": 2 * xh + other_c}, device_id_type=MESH
            )

        return carry

    lax.fori_loop(0, 32, greet, 0)
    pl.semaphore_wait(barrier, 31)

    def piece(kind, j):
        cols = pl.ds(j * HD, HD)
        zt = 2 * j + c
        if kind == "k":
            return k_in.at[:, cols], kv.at[0, 2 * z + x], k_send.at[j], kv_recv.at[z], zt, 0
        if kind == "v":
            return v_in.at[:, cols], kv.at[1, 2 * z + x], v_send.at[j], kv_recv.at[z], zt, 1
        a = int(kind[1])
        return q_in.at[pl.ds(a * HALF, HALF), cols], qu.at[z], q_send.at[j, a], q_recv.at[z], zt, a

    def each_piece(do):
        for kind in ("k", "v", "q0", "q1"):
            for j in range(4):
                do(*piece(kind, j))

    def start_piece(src, dst, send, recv, zt, core):
        here = jnp.logical_and(zt == z, c == core)

        @pl.when(here)
        def _():
            pltpu.make_async_copy(src, dst, recv).start()

        @pl.when(jnp.logical_not(here))
        def _():
            remote(src, dst, send, recv, at(zt, x, core)).start()

    def sent_piece(src, dst, send, recv, zt, core):
        @pl.when(jnp.logical_not(jnp.logical_and(zt == z, c == core)))
        def _():
            remote(src, dst, send, recv, at(zt, x, core)).wait_send()

    cols5 = pl.ds(4 * HD, HD)

    def swap_copies():
        k_dst = 2 * z + x
        return (
            (k_in.at[:, cols5], kv5.at[k_dst, 0], 0),
            (v_in.at[:, cols5], kv5.at[k_dst, 1], 1),
            (q_in.at[:, cols5], q5, 2),
        )

    same = c == x

    def start_swap():
        for src, dst, n in swap_copies():

            @pl.when(same)
            def _():
                pltpu.make_async_copy(src, dst, f_recv.at[n]).start()

            @pl.when(jnp.logical_not(same))
            def _():
                remote(src, dst, f_send.at[n], f_recv.at[n], at(z, 1 - x, 1 - c)).start()

    def sent_swap():
        @pl.when(jnp.logical_not(same))
        def _():
            for src, dst, n in swap_copies():
                remote(src, dst, f_send.at[n], f_recv.at[n], at(z, 1 - x, 1 - c)).wait_send()

    start_swap()
    each_piece(start_piece)
    lg5[...] = jnp.zeros((8, HD), jnp.float32)

    ids = ids_ref[...]
    starts = [jnp.sum(jnp.sum(jnp.where(ids < n, 1.0, 0.0), axis=0, keepdims=True), axis=1, keepdims=True) for n in (1, 2, 3)]

    def clip_of(first, rows):
        pos = (first + lax.broadcasted_iota(jnp.int32, (rows, HD), 0)).astype(jnp.float32)
        clip = jnp.zeros((rows, HD), jnp.float32)
        for s in starts:
            clip = clip + jnp.where(pos >= s, 1.0, 0.0)
        return clip, lax.broadcasted_iota(jnp.int32, (rows, HD), 1).astype(jnp.float32)

    def fill(b, carry):
        clip, lane = clip_of(b * ROWS, ROWS)
        mk[b] = jnp.where(lane == clip, 0.0, jnp.where(lane < 4.0, 1.0, 0.0)).astype(jnp.bfloat16)
        return carry

    def block_in(src):
        return kv.at[c, 2 * src + x]

    def to_x(src):
        return remote(block_in(src), block_in(src), x_send.at[src], x_recv.at[src], at(z, 1 - x, c))

    def to_core(b):
        return remote(kv.at[c, b], kv.at[c, b], c_send.at[b], c_recv.at[b], at(z, x, 1 - c))

    def relay(d):
        src = (z + d + NZ) % NZ
        arrived(block_in(src), kv_recv.at[src])
        to_x(src).start()
        to_core(2 * src + x).start()

    def relay_x(d):
        src = (z + d + NZ) % NZ
        b = 2 * src + 1 - x
        arrived(kv.at[c, b], x_recv.at[src])
        to_core(b).start()

    def c5_copy(zz):
        b = 2 * zz + c
        return remote(kv5.at[b], kv5.at[b], c5_send.at[zz], c5_recv.at[b], at(z, x, 1 - c))

    def right(s):
        b = 2 * (z - s + 1) + c
        return remote(kv5.at[b], kv5.at[b], ch_send.at[0, s - 1], chl_recv.at[s - 1], at((z + 1) % NZ, x, c))

    def left(s):
        b = 2 * (z + s - 1) + c
        return remote(kv5.at[b], kv5.at[b], ch_send.at[1, s - 1], chr_recv.at[s - 1], at((z + NZ - 1) % NZ, x, c))

    def goes_right(s):
        return jnp.logical_and(z + 1 < NZ, z - s + 1 >= 0)

    def goes_left(s):
        return jnp.logical_and(z - 1 >= 0, z + s - 1 < NZ)

    lax.fori_loop(0, 16, fill, 0)
    order = (0, 1, -1, 2, -2, 3, -3, 4)
    for d in order[:3]:
        relay(d)
    arrived(kv5.at[kb5, 0], f_recv.at[0])
    arrived(kv5.at[kb5, 1], f_recv.at[1])
    c5_copy(z).start()

    @pl.when(goes_right(1))
    def _():
        right(1).start()

    @pl.when(goes_left(1))
    def _():
        left(1).start()

    for d in order[3:]:
        relay(d)
    for d in order:
        relay_x(d)
    for src in range(NZ):
        arrived(qu.at[src], q_recv.at[src])
    for b in range(16):
        arrived(kv.at[1 - c, b], c_recv.at[b])

    def chain(s):
        @pl.when(z - s >= 0)
        def _():
            b = 2 * (z - s) + c
            arrived(kv5.at[b], chl_recv.at[s - 1])
            c5_copy(z - s).start()

        if s < 3:

            @pl.when(goes_right(s + 1))
            def _():
                right(s + 1).start()

        @pl.when(z + s < NZ)
        def _():
            b = 2 * (z + s) + c
            arrived(kv5.at[b], chr_recv.at[s - 1])
            c5_copy(z + s).start()

        if s < 3:

            @pl.when(goes_left(s + 1))
            def _():
                left(s + 1).start()

    ones = jnp.ones((ROWS, HD), jnp.bfloat16)

    def attend(q, first, block, k_of, v_of):
        clip, lane = clip_of(first, HALF)
        mq = jnp.where(lane == clip, -APART, 0.0).astype(jnp.bfloat16)
        qa = jnp.concatenate([q, mq], axis=1)
        m_ref[...] = jnp.full((HALF, HD), -1e30, jnp.float32)
        acc_ref[...] = jnp.zeros((HALF, 2 * HD), jnp.float32)

        def step(b, carry):
            ka = jnp.concatenate([k_of(b), mk[b]], axis=1)
            s = lax.dot_general(qa, ka, (((1,), (1,)), ((), ())), preferred_element_type=jnp.float32)
            m_old = m_ref[...]
            m_new = jnp.maximum(m_old, jnp.max(s, axis=1, keepdims=True))
            alpha = jnp.exp2((m_old - m_new) * TO_EXP2)
            p = jnp.exp2((s - jnp.concatenate([m_new] * (ROWS // HD), axis=1)) * TO_EXP2)
            va = jnp.concatenate([v_of(b), ones], axis=1)
            pv = jnp.dot(p.astype(jnp.bfloat16), va, preferred_element_type=jnp.float32)
            acc_ref[...] = acc_ref[...] * jnp.concatenate([alpha, alpha], axis=1) + pv
            m_ref[...] = m_new
            return carry

        lax.fori_loop(jnp.maximum(block - REACH, 0), jnp.minimum(block + REACH + 1, 2 * NZ), step, 0)
        total = acc_ref[:, HD:]
        out = (acc_ref[:, :HD] / total).astype(jnp.bfloat16)
        log_total = m_ref[...] * SCALE + jnp.log(total)
        return out, jnp.transpose(log_total)[0:1, :]

    cols_out = pl.ds(pl.multiple_of(i_head * HD, HD), HD)

    def o_copy(zq):
        return remote(
            ou.at[zq], att.at[pl.ds(pl.multiple_of(c * HALF, HALF), HALF), cols_out],
            o_send.at[zq], o_recv.at[i_head, c], at(zq, x, g),
        )

    def o_home(zq):
        return jnp.logical_and(zq == z, c == g)

    def send_o(zq):
        @pl.when(o_home(zq))
        def _():
            pltpu.make_async_copy(
                ou.at[zq], att.at[pl.ds(pl.multiple_of(c * HALF, HALF), HALF), cols_out], o_recv.at[i_head, c]
            ).start()

        @pl.when(jnp.logical_not(o_home(zq)))
        def _():
            o_copy(zq).start()

    def chunk(zq, carry):
        block = 2 * zq + x
        out, row = attend(qu[zq], block * ROWS + c * HALF, block, lambda b: kv[0, b], lambda b: kv[1, b])
        ou[zq] = out
        lg[pl.ds(2 * zq, 1), :] = row[:, :HD]
        lg[pl.ds(2 * zq + 1, 1), :] = row[:, HD:]

        @pl.when(zq > 0)
        def _():
            send_o(jnp.maximum(zq - 1, 0))

        return carry

    lax.fori_loop(0, 3, chunk, 0)
    chain(1)
    lax.fori_loop(3, 6, chunk, 0)
    chain(2)
    lax.fori_loop(6, 8, chunk, 0)
    chain(3)
    send_o(7)

    def lg_copy(t):
        return remote(lg, lg_all.at[i_head, 2 * x + c], lg_send.at[t], lg_recv.at[i_head, 2 * x + c], {"seq": t, "head": 2 * xh + g})

    def lg_here(t):
        return jnp.logical_and(t == seq, c == g)

    def send_lg(t, carry):
        @pl.when(lg_here(t))
        def _():
            pltpu.make_async_copy(lg, lg_all.at[i_head, 2 * x + c], lg_recv.at[i_head, 2 * x + c]).start()

        @pl.when(jnp.logical_not(lg_here(t)))
        def _():
            lg_copy(t).start()

        return carry

    arrived(q5, f_recv.at[2])
    for d in range(-3, 4):

        @pl.when(jnp.logical_and(z + d >= 0, z + d < NZ))
        def _():
            b = 2 * (z + d) + 1 - c
            arrived(kv5.at[b], c5_recv.at[b])

    for h in range(2):
        out, row = attend(
            q5[h * HALF : (h + 1) * HALF, :], kb5 * ROWS + h * HALF, kb5, lambda b: kv5[b, 0], lambda b: kv5[b, 1]
        )
        o5[h * HALF : (h + 1) * HALF, :] = out
        lg5[2 * h : 2 * h + 1, :] = row[:, :HD]
        lg5[2 * h + 1 : 2 * h + 2, :] = row[:, HD:]
        if h == 0:
            lax.fori_loop(0, 16, send_lg, 0)

    def find(b, state):
        count, found = state[0], state[1:]
        mine = plan_ref[b] == seq
        found = tuple(jnp.where(jnp.logical_and(mine, count == n), b, f) for n, f in enumerate(found))
        return (count + jnp.where(mine, 1, 0), *found)

    found = lax.fori_loop(0, 64, find, (0, 0, 0, 0, 0))[1:]

    def lg5_copy(t):
        return remote(lg5, lg5_all.at[kb5], lg5_send.at[t], lg5_recv.at[kb5], {"seq": t, "head": 2 * xh + x})

    def lg5_here(t):
        return jnp.logical_and(t == seq, c == x)

    def send_lg5(t, carry):
        @pl.when(lg5_here(t))
        def _():
            pltpu.make_async_copy(lg5, lg5_all.at[kb5], lg5_recv.at[kb5]).start()

        @pl.when(jnp.logical_not(lg5_here(t)))
        def _():
            lg5_copy(t).start()

        return carry

    lax.fori_loop(0, 16, send_lg5, 0)
    o5_dst = att.at[:, cols5]

    @pl.when(same)
    def _():
        pltpu.make_async_copy(o5, o5_dst, o5_recv).start()

    @pl.when(jnp.logical_not(same))
    def _():
        remote(o5, o5_dst, o5_send, o5_recv, at(z, 1 - x, 1 - c)).start()

    each_piece(sent_piece)
    sent_swap()
    for src in range(NZ):
        to_x(src).wait_send()
    for b in range(16):
        to_core(b).wait_send()
    for d in range(-3, 4):

        @pl.when(jnp.logical_and(z + d >= 0, z + d < NZ))
        def _():
            c5_copy(z + d).wait_send()

    for s in (1, 2, 3):

        @pl.when(goes_right(s))
        def _():
            right(s).wait_send()

        @pl.when(goes_left(s))
        def _():
            left(s).wait_send()

    for zq in range(NZ):

        @pl.when(jnp.logical_not(o_home(zq)))
        def _():
            o_copy(zq).wait_send()

    def sent_lg(t, carry):
        @pl.when(jnp.logical_not(lg_here(t)))
        def _():
            lg_copy(t).wait_send()

        @pl.when(jnp.logical_not(lg5_here(t)))
        def _():
            lg5_copy(t).wait_send()

        return carry

    lax.fori_loop(0, 16, sent_lg, 0)

    @pl.when(jnp.logical_not(same))
    def _():
        remote(o5, o5_dst, o5_send, o5_recv, at(z, 1 - x, 1 - c)).wait_send()

    for i in range(4):
        for w in range(4):
            arrived(lg_all.at[i, w], lg_recv.at[i, w])
    for b in range(16):
        arrived(lg5_all.at[b], lg5_recv.at[b])
    for n, b in enumerate(found):
        w = (b // 2) % 4
        row = 2 * (b // 8) + b % 2
        for i in range(4):
            lg_out[i : i + 1, n * HD : (n + 1) * HD] = lg_all[i, w, pl.ds(row, 1), :]
        lg_out[4:5, n * HD : (n + 1) * HD] = lg5_all[b // 4, pl.ds(b % 4, 1), :]
    for i in range(4):
        for a in range(2):
            arrived(att.at[pl.ds(a * HALF, HALF), pl.ds(i * HD, HD)], o_recv.at[i, a])
    arrived(o5_dst, o5_recv)


def shards(queries, keys, values, clip_ids, plan):
    vmem = pl.BlockSpec(memory_space=pltpu.VMEM)
    anywhere = pl.BlockSpec(memory_space=pl.ANY)
    bf16, f32 = jnp.bfloat16, jnp.float32
    dma = pltpu.SemaphoreType.DMA
    return pl.pallas_call(
        kernel,
        out_shape=(jax.ShapeDtypeStruct((ROWS, 5 * HD), bf16), jax.ShapeDtypeStruct((5, ROWS), f32)),
        in_specs=[anywhere, anywhere, anywhere, vmem, pl.BlockSpec(memory_space=pltpu.SMEM)],
        out_specs=(vmem, vmem),
        scratch_shapes=[
            pltpu.VMEM((2, 2 * NZ, ROWS, HD), bf16),
            pltpu.VMEM((NZ, HALF, HD), bf16),
            pltpu.VMEM((NZ, HALF, HD), bf16),
            pltpu.VMEM((2 * NZ, 2, ROWS, HD), bf16),
            pltpu.VMEM((ROWS, HD), bf16),
            pltpu.VMEM((ROWS, HD), bf16),
            pltpu.VMEM((2 * NZ, ROWS, HD), bf16),
            pltpu.VMEM((HALF, HD), f32),
            pltpu.VMEM((HALF, 2 * HD), f32),
            pltpu.VMEM((2 * NZ, HD), f32),
            pltpu.VMEM((8, HD), f32),
            pltpu.VMEM((4, 4, 2 * NZ, HD), f32),
            pltpu.VMEM((2 * NZ, 8, HD), f32),
            dma((4, 2)), dma((4,)), dma((4,)), dma((NZ,)), dma((2 * NZ,)), dma((3,)), dma((2, 3)), dma((NZ,)),
            dma((NZ,)), dma, dma((16,)), dma((16,)),
            dma((NZ,)), dma((NZ,)), dma((NZ,)), dma((2 * NZ,)), dma((3,)), dma((3,)), dma((3,)), dma((2 * NZ,)),
            dma((4, 2)), dma, dma((4, 4)), dma((16,)),
        ],
        compiler_params=pltpu.CompilerParams(collective_id=0, has_side_effects=True, vmem_limit_bytes=48 << 20),
        name="clips",
    )(queries, keys, values, clip_ids.reshape(64, HD), plan)


def solution(mesh):
    return jax.shard_map(
        shards,
        mesh=mesh,
        in_specs=(
            P(("req", "seq"), "head"),
            P(("req", "seq"), "head"),
            P(("req", "seq"), "head"),
            P("req"),
            P("req"),
        ),
        out_specs=(P(("req", "seq"), "head"), P("head", ("req", "seq"))),
        check_vma=False,
    )
```

```python
import functools

import jax
import jax.numpy as jnp
from jax import lax
from jax.experimental import pallas as pl
from jax.experimental.pallas import tpu as pltpu
from jax.sharding import PartitionSpec as P

HD = 128
ROWS = 512
HALF = 256
NZ = 8
APART = 32768.0
SCALE = 1.0 / HD**0.5
TO_EXP2 = 1.4426950408889634 * SCALE
MESH = pl.DeviceIdType.MESH


def kernel(
    q_in, k_in, v_in, ids_ref, plan_ref,
    att, lg_out,
    kv, qu, ou, kv5, q5, o5, mk, mq, m_all, acc_all, lg, lg5, lg_all, lg5_all,
    q_send, k_send, v_send, x_send, c_send, f_send, ch_send, c5_send, o_send, o5_send, lg_send, lg5_send,
    q_recv, kv_recv, x_recv, c_recv, f_recv, chl_recv, chr_recv, c5_recv, o_recv, o5_recv, lg_recv, lg5_recv,
):
    seq = lax.axis_index("seq")
    head = lax.axis_index("head")
    z, x = seq // 2, seq % 2
    xh, c = head // 2, head % 2
    g, i_head = z % 2, z // 2
    kb5 = 2 * z + c

    def at(zz, xx, cc):
        return {"seq": 2 * zz + xx, "head": 2 * xh + cc}

    def remote(src, dst, send, recv, where):
        return pltpu.make_async_remote_copy(
            src_ref=src, dst_ref=dst, send_sem=send, recv_sem=recv, device_id=where, device_id_type=MESH
        )

    def arrived(dst, recv):
        remote(dst, dst, recv, recv, at(z, x, 1 - c)).wait_recv()

    barrier = pltpu.get_barrier_semaphore()

    def greet(t, carry):
        other_seq, other_c = t // 2, t % 2

        @pl.when(jnp.logical_or(other_seq != seq, other_c != c))
        def _():
            pl.semaphore_signal(
                barrier, inc=1, device_id={"seq": other_seq, "head": 2 * xh + other_c}, device_id_type=MESH
            )

        return carry

    lax.fori_loop(0, 32, greet, 0)
    pl.semaphore_wait(barrier, 31)

    odd = (z + c) % 2

    def piece(kind, n):
        d = (odd, 2 - 3 * odd, 5 * odd - 2, 4 - 7 * odd)[n]
        zt = (z + d + NZ) % NZ
        cols = pl.ds(pl.multiple_of((zt // 2) * HD, HD), HD)
        if kind == "k":
            return k_in.at[:, cols], kv.at[0, 2 * z + x], k_send.at[n], kv_recv.at[z], zt, 0
        if kind == "v":
            return v_in.at[:, cols], kv.at[1, 2 * z + x], v_send.at[n], kv_recv.at[z], zt, 1
        return q_in.at[:, cols], qu.at[z // 2], q_send.at[n], q_recv.at[z // 2], zt, z % 2

    def each_piece(do):
        for n in range(4):
            for kind in ("k", "v", "q"):
                do(*piece(kind, n))

    def start_piece(src, dst, send, recv, zt, core):
        here = jnp.logical_and(zt == z, c == core)

        @pl.when(here)
        def _():
            pltpu.make_async_copy(src, dst, recv).start()

        @pl.when(jnp.logical_not(here))
        def _():
            remote(src, dst, send, recv, at(zt, x, core)).start()

    def sent_piece(src, dst, send, recv, zt, core):
        @pl.when(jnp.logical_not(jnp.logical_and(zt == z, c == core)))
        def _():
            remote(src, dst, send, recv, at(zt, x, core)).wait_send()

    cols5 = pl.ds(4 * HD, HD)

    def swap_copies():
        k_dst = 2 * z + x
        return (
            (k_in.at[:, cols5], kv5.at[k_dst, 0], 0),
            (v_in.at[:, cols5], kv5.at[k_dst, 1], 1),
            (q_in.at[:, cols5], q5, 2),
        )

    same = c == x

    def start_swap():
        for src, dst, n in swap_copies():

            @pl.when(same)
            def _():
                pltpu.make_async_copy(src, dst, f_recv.at[n]).start()

            @pl.when(jnp.logical_not(same))
            def _():
                remote(src, dst, f_send.at[n], f_recv.at[n], at(z, 1 - x, 1 - c)).start()

    def sent_swap():
        @pl.when(jnp.logical_not(same))
        def _():
            for src, dst, n in swap_copies():
                remote(src, dst, f_send.at[n], f_recv.at[n], at(z, 1 - x, 1 - c)).wait_send()

    start_swap()
    each_piece(start_piece)
    lg5[...] = jnp.zeros((8, HD), jnp.float32)

    ids = ids_ref[...]
    starts = [jnp.sum(jnp.sum(jnp.where(ids < n, 1.0, 0.0), axis=0, keepdims=True), axis=1, keepdims=True) for n in (1, 2, 3)]

    def clip_of(block):
        pos = (block * ROWS + lax.broadcasted_iota(jnp.int32, (ROWS, HD), 0)).astype(jnp.float32)
        clip = jnp.zeros((ROWS, HD), jnp.float32)
        for s in starts:
            clip = clip + jnp.where(pos >= s, 1.0, 0.0)
        return clip, lax.broadcasted_iota(jnp.int32, (ROWS, HD), 1).astype(jnp.float32)

    def fill(b, carry):
        clip, lane = clip_of(b)
        mk[b] = jnp.where(lane == clip, 0.0, jnp.where(lane < 4.0, 1.0, 0.0)).astype(jnp.bfloat16)
        return carry

    def fill_q(n, carry):
        clip, lane = clip_of(jnp.where(n == 4, kb5, 2 * (2 * n + c) + x))
        mq[n] = jnp.where(lane == clip, -APART, 0.0).astype(jnp.bfloat16)
        m_all[n] = jnp.full((ROWS, HD), -1e30, jnp.float32)
        acc_all[n] = jnp.zeros((ROWS, 2 * HD), jnp.float32)
        return carry

    def block_in(src):
        return kv.at[c, 2 * src + x]

    def to_x(src):
        return remote(block_in(src), block_in(src), x_send.at[src], x_recv.at[src], at(z, 1 - x, c))

    def to_core(b):
        return remote(kv.at[c, b], kv.at[c, b], c_send.at[b], c_recv.at[b], at(z, x, 1 - c))

    def relay(src):
        arrived(block_in(src), kv_recv.at[src])
        to_x(src).start()
        to_core(2 * src + x).start()

    def relay_x(src):
        b = 2 * src + 1 - x
        arrived(kv.at[c, b], x_recv.at[src])
        to_core(b).start()

    def c5_copy(zz):
        b = 2 * zz + c
        return remote(kv5.at[b], kv5.at[b], c5_send.at[zz], c5_recv.at[b], at(z, x, 1 - c))

    def right(s):
        b = 2 * (z - s + 1) + c
        return remote(kv5.at[b], kv5.at[b], ch_send.at[0, s - 1], chl_recv.at[s - 1], at((z + 1) % NZ, x, c))

    def left(s):
        b = 2 * (z + s - 1) + c
        return remote(kv5.at[b], kv5.at[b], ch_send.at[1, s - 1], chr_recv.at[s - 1], at((z + NZ - 1) % NZ, x, c))

    def goes_right(s):
        return jnp.logical_and(z + 1 < NZ, z - s + 1 >= 0)

    def goes_left(s):
        return jnp.logical_and(z - 1 >= 0, z + s - 1 < NZ)

    def chain(s):
        @pl.when(z - s >= 0)
        def _():
            arrived(kv5.at[2 * (z - s) + c], chl_recv.at[s - 1])
            c5_copy(z - s).start()

        if s < 3:

            @pl.when(goes_right(s + 1))
            def _():
                right(s + 1).start()

        @pl.when(z + s < NZ)
        def _():
            arrived(kv5.at[2 * (z + s) + c], chr_recv.at[s - 1])
            c5_copy(z + s).start()

        if s < 3:

            @pl.when(goes_left(s + 1))
            def _():
                left(s + 1).start()

    def offset(t):
        return ((t + 1) // 2) * (2 * (t % 2) - 1)

    def source(t):
        return (z + offset(t) + NZ) % NZ

    ones = jnp.ones((2 * ROWS, HD), jnp.bfloat16)

    def tile(n, q, zk, k_of, v_of):
        keys = [jnp.concatenate([k_of(2 * zk + l), mk[2 * zk + l]], axis=1) for l in range(2)]
        va = jnp.concatenate([jnp.concatenate([v_of(2 * zk), v_of(2 * zk + 1)], axis=0), ones], axis=1)
        for h in range(2):
            part = slice(h * HALF, (h + 1) * HALF)
            qa = jnp.concatenate([q[part, :], mq[n, part, :]], axis=1)
            scores = [
                lax.dot_general(qa, k, (((1,), (1,)), ((), ())), preferred_element_type=jnp.float32) for k in keys
            ]
            top = functools.reduce(
                jnp.maximum, [s[:, l * HD : (l + 1) * HD] for s in scores for l in range(ROWS // HD)]
            )
            m_old = m_all[n, part, :]
            m_new = jnp.maximum(m_old, jnp.max(top, axis=1, keepdims=True))
            alpha = jnp.exp2((m_old - m_new) * TO_EXP2)
            m_wide = jnp.concatenate([m_new] * (ROWS // HD), axis=1)
            p = jnp.concatenate([jnp.exp2((s - m_wide) * TO_EXP2).astype(jnp.bfloat16) for s in scores], axis=1)
            pv = jnp.dot(p, va, preferred_element_type=jnp.float32)
            acc_all[n, part, :] = acc_all[n, part, :] * jnp.concatenate([alpha, alpha], axis=1) + pv
            m_all[n, part, :] = m_new

    def finish(n):
        total = acc_all[n, :, HD:]
        out = (acc_all[n, :, :HD] / total).astype(jnp.bfloat16)
        rows = jnp.transpose(m_all[n] * SCALE + jnp.log(total))[0:1, :]
        return out, [rows[:, r * HD : (r + 1) * HD] for r in range(ROWS // HD)]

    cols_out = pl.ds(pl.multiple_of(i_head * HD, HD), HD)

    def o_dst():
        return att.at[:, cols_out]

    def o_copy(n):
        return remote(ou.at[n], o_dst(), o_send.at[n], o_recv.at[i_head], at(2 * n + c, x, g))

    def o_home(n):
        return jnp.logical_and(2 * n + c == z, c == g)

    def send_o(n):
        @pl.when(o_home(n))
        def _():
            pltpu.make_async_copy(ou.at[n], o_dst(), o_recv.at[i_head]).start()

        @pl.when(jnp.logical_not(o_home(n)))
        def _():
            o_copy(n).start()

    lax.fori_loop(0, 16, fill, 0)
    lax.fori_loop(0, 5, fill_q, 0)
    relay(source(0))
    relay_x(source(0))

    def stage(j, carry):
        s_j = source(j)

        @pl.when(j < 7)
        def _():
            relay(source(jnp.minimum(j + 1, 7)))

        @pl.when(j == 1)
        def _():
            arrived(kv5.at[kb5, 0], f_recv.at[0])
            arrived(kv5.at[kb5, 1], f_recv.at[1])
            arrived(q5, f_recv.at[2])
            c5_copy(z).start()

            @pl.when(goes_right(1))
            def _():
                right(1).start()

            @pl.when(goes_left(1))
            def _():
                left(1).start()

        for l in range(2):
            arrived(kv.at[1 - c, 2 * s_j + l], c_recv.at[2 * s_j + l])

        @pl.when(s_j % 2 == c)
        def _():
            arrived(qu.at[s_j // 2], q_recv.at[s_j // 2])

        @pl.when(j < 7)
        def _():
            relay_x(source(jnp.minimum(j + 1, 7)))

        return carry

    lax.fori_loop(0, 8, stage, 0)

    def chunk(n, carry):
        zq = 2 * n + c

        def step(zk, inner):
            tile(n, qu.at[n], zk, lambda b: kv[0, b], lambda b: kv[1, b])
            return inner

        lax.fori_loop(jnp.maximum(zq - 3, 0), jnp.minimum(zq + 4, NZ), step, 0)
        out, rows = finish(n)
        ou[n] = out
        for r in range(4):
            lg[pl.ds(4 * n + r, 1), :] = rows[r]

        @pl.when(n > 0)
        def _():
            send_o(jnp.maximum(n - 1, 0))

        return carry

    chain(1)
    lax.fori_loop(0, 1, chunk, 0)
    chain(2)
    lax.fori_loop(1, 2, chunk, 0)
    chain(3)
    lax.fori_loop(2, 4, chunk, 0)
    send_o(3)

    def lg_copy(t):
        return remote(lg, lg_all.at[i_head, 2 * x + c], lg_send.at[t], lg_recv.at[i_head, 2 * x + c], {"seq": t, "head": 2 * xh + g})

    def lg_here(t):
        return jnp.logical_and(t == seq, c == g)

    def send_lg(t, carry):
        @pl.when(lg_here(t))
        def _():
            pltpu.make_async_copy(lg, lg_all.at[i_head, 2 * x + c], lg_recv.at[i_head, 2 * x + c]).start()

        @pl.when(jnp.logical_not(lg_here(t)))
        def _():
            lg_copy(t).start()

        return carry

    lax.fori_loop(0, 16, send_lg, 0)
    def own_there(t, carry):
        zk = z + offset(t)

        @pl.when(jnp.logical_and(zk >= 0, zk < NZ))
        def _():
            b = 2 * zk + 1 - c
            arrived(kv5.at[b], c5_recv.at[b])

        return carry

    def own(zk, carry):
        tile(4, q5, zk, lambda b: kv5[b, 0], lambda b: kv5[b, 1])
        return carry

    lax.fori_loop(0, 7, own_there, 0)
    lax.fori_loop(jnp.maximum(z - 3, 0), jnp.minimum(z + 4, NZ), own, 0)
    out, rows = finish(4)
    o5[...] = out
    for r in range(4):
        lg5[r : r + 1, :] = rows[r]

    def find(b, state):
        count, found = state[0], state[1:]
        mine = plan_ref[b] == seq
        found = tuple(jnp.where(jnp.logical_and(mine, count == n), b, f) for n, f in enumerate(found))
        return (count + jnp.where(mine, 1, 0), *found)

    found = lax.fori_loop(0, 64, find, (0, 0, 0, 0, 0))[1:]

    def lg5_copy(t):
        return remote(lg5, lg5_all.at[kb5], lg5_send.at[t], lg5_recv.at[kb5], {"seq": t, "head": 2 * xh + x})

    def lg5_here(t):
        return jnp.logical_and(t == seq, c == x)

    def send_lg5(t, carry):
        @pl.when(lg5_here(t))
        def _():
            pltpu.make_async_copy(lg5, lg5_all.at[kb5], lg5_recv.at[kb5]).start()

        @pl.when(jnp.logical_not(lg5_here(t)))
        def _():
            lg5_copy(t).start()

        return carry

    lax.fori_loop(0, 16, send_lg5, 0)
    o5_dst = att.at[:, cols5]

    @pl.when(same)
    def _():
        pltpu.make_async_copy(o5, o5_dst, o5_recv).start()

    @pl.when(jnp.logical_not(same))
    def _():
        remote(o5, o5_dst, o5_send, o5_recv, at(z, 1 - x, 1 - c)).start()

    each_piece(sent_piece)
    sent_swap()
    for src in range(NZ):
        to_x(src).wait_send()
    for b in range(16):
        to_core(b).wait_send()
    for d in range(-3, 4):

        @pl.when(jnp.logical_and(z + d >= 0, z + d < NZ))
        def _():
            c5_copy(z + d).wait_send()

    for s in (1, 2, 3):

        @pl.when(goes_right(s))
        def _():
            right(s).wait_send()

        @pl.when(goes_left(s))
        def _():
            left(s).wait_send()

    for n in range(4):

        @pl.when(jnp.logical_not(o_home(n)))
        def _(n=n):
            o_copy(n).wait_send()

    def sent_lg(t, carry):
        @pl.when(jnp.logical_not(lg_here(t)))
        def _():
            lg_copy(t).wait_send()

        @pl.when(jnp.logical_not(lg5_here(t)))
        def _():
            lg5_copy(t).wait_send()

        return carry

    lax.fori_loop(0, 16, sent_lg, 0)

    @pl.when(jnp.logical_not(same))
    def _():
        remote(o5, o5_dst, o5_send, o5_recv, at(z, 1 - x, 1 - c)).wait_send()

    for i in range(4):
        for w in range(4):
            arrived(lg_all.at[i, w], lg_recv.at[i, w])
    for b in range(16):
        arrived(lg5_all.at[b], lg5_recv.at[b])
    for n, b in enumerate(found):
        w = 2 * ((b // 4) % 2) + (b // 8) % 2
        row = 4 * (b // 16) + b % 4
        for i in range(4):
            lg_out[i : i + 1, n * HD : (n + 1) * HD] = lg_all[i, w, pl.ds(row, 1), :]
        lg_out[4:5, n * HD : (n + 1) * HD] = lg5_all[b // 4, pl.ds(b % 4, 1), :]
    for i in range(4):
        arrived(att.at[:, pl.ds(i * HD, HD)], o_recv.at[i])
    arrived(o5_dst, o5_recv)


def shards(queries, keys, values, clip_ids, plan):
    vmem = pl.BlockSpec(memory_space=pltpu.VMEM)
    anywhere = pl.BlockSpec(memory_space=pl.ANY)
    bf16, f32 = jnp.bfloat16, jnp.float32
    dma = pltpu.SemaphoreType.DMA
    return pl.pallas_call(
        kernel,
        out_shape=(jax.ShapeDtypeStruct((ROWS, 5 * HD), bf16), jax.ShapeDtypeStruct((5, ROWS), f32)),
        in_specs=[anywhere, anywhere, anywhere, vmem, pl.BlockSpec(memory_space=pltpu.SMEM)],
        out_specs=(vmem, vmem),
        scratch_shapes=[
            pltpu.VMEM((2, 2 * NZ, ROWS, HD), bf16),
            pltpu.VMEM((4, ROWS, HD), bf16),
            pltpu.VMEM((4, ROWS, HD), bf16),
            pltpu.VMEM((2 * NZ, 2, ROWS, HD), bf16),
            pltpu.VMEM((ROWS, HD), bf16),
            pltpu.VMEM((ROWS, HD), bf16),
            pltpu.VMEM((2 * NZ, ROWS, HD), bf16),
            pltpu.VMEM((5, ROWS, HD), bf16),
            pltpu.VMEM((5, ROWS, HD), f32),
            pltpu.VMEM((5, ROWS, 2 * HD), f32),
            pltpu.VMEM((2 * NZ, HD), f32),
            pltpu.VMEM((8, HD), f32),
            pltpu.VMEM((4, 4, 2 * NZ, HD), f32),
            pltpu.VMEM((2 * NZ, 8, HD), f32),
            dma((4,)), dma((4,)), dma((4,)), dma((NZ,)), dma((2 * NZ,)), dma((3,)), dma((2, 3)), dma((NZ,)),
            dma((4,)), dma, dma((16,)), dma((16,)),
            dma((4,)), dma((NZ,)), dma((NZ,)), dma((2 * NZ,)), dma((3,)), dma((3,)), dma((3,)), dma((2 * NZ,)),
            dma((4,)), dma, dma((4, 4)), dma((16,)),
        ],
        compiler_params=pltpu.CompilerParams(collective_id=0, has_side_effects=True, vmem_limit_bytes=67043328),
        name="clips",
    )(queries, keys, values, clip_ids.reshape(64, HD), plan)


def solution(mesh):
    return jax.shard_map(
        shards,
        mesh=mesh,
        in_specs=(
            P(("req", "seq"), "head"),
            P(("req", "seq"), "head"),
            P(("req", "seq"), "head"),
            P("req"),
            P("req"),
        ),
        out_specs=(P(("req", "seq"), "head"), P("head", ("req", "seq"))),
        check_vma=False,
    )
```

```python
import functools

import jax
import jax.numpy as jnp
from jax import lax
from jax.experimental import pallas as pl
from jax.experimental.pallas import tpu as pltpu
from jax.sharding import PartitionSpec as P

HD = 128
ROWS = 512
HALF = 256
NZ = 8
APART = 32768.0
SCALE = 1.0 / HD**0.5
TO_EXP2 = 1.4426950408889634 * SCALE
MESH = pl.DeviceIdType.MESH


def kernel(
    q_in, k_in, v_in, ids_ref, plan_ref,
    att, lg_out,
    kv, qu, ou, kv5, q5, o5, mk, mq, m_all, acc_all, lg, lg5, lg_all, lg5_all,
    q_send, k_send, v_send, x_send, c_send, f_send, ch_send, c5_send, o_send, o5_send, lg_send, lg5_send,
    q_recv, kv_recv, x_recv, c_recv, f_recv, chl_recv, chr_recv, c5_recv, o_recv, o5_recv, lg_recv, lg5_recv,
):
    seq = lax.axis_index("seq")
    head = lax.axis_index("head")
    z, x = seq // 2, seq % 2
    xh, c = head // 2, head % 2
    g, i_head = z % 2, z // 2
    kb5 = 2 * z + c

    def at(zz, xx, cc):
        return {"seq": 2 * zz + xx, "head": 2 * xh + cc}

    def remote(src, dst, send, recv, where):
        return pltpu.make_async_remote_copy(
            src_ref=src, dst_ref=dst, send_sem=send, recv_sem=recv, device_id=where, device_id_type=MESH
        )

    def arrived(dst, recv):
        remote(dst, dst, recv, recv, at(z, x, 1 - c)).wait_recv()

    barrier = pltpu.get_barrier_semaphore()

    def greet(t, carry):
        other_seq, other_c = t // 2, t % 2

        @pl.when(jnp.logical_or(other_seq != seq, other_c != c))
        def _():
            pl.semaphore_signal(
                barrier, inc=1, device_id={"seq": other_seq, "head": 2 * xh + other_c}, device_id_type=MESH
            )

        return carry

    lax.fori_loop(0, 32, greet, 0)
    pl.semaphore_wait(barrier, 31)

    odd = (z + c) % 2

    def piece(kind, n):
        d = (odd, 2 - 3 * odd, 5 * odd - 2, 4 - 7 * odd)[n]
        zt = (z + d + NZ) % NZ
        cols = pl.ds(pl.multiple_of((zt // 2) * HD, HD), HD)
        if kind == "k":
            return k_in.at[:, cols], kv.at[0, 2 * z + x], k_send.at[n], kv_recv.at[z], zt, 0
        if kind == "v":
            return v_in.at[:, cols], kv.at[1, 2 * z + x], v_send.at[n], kv_recv.at[z], zt, 1
        return q_in.at[:, cols], qu.at[z // 2], q_send.at[n], q_recv.at[z // 2], zt, z % 2

    def each_piece(do):
        for n in range(4):
            for kind in ("k", "v", "q"):
                do(*piece(kind, n))

    def start_piece(src, dst, send, recv, zt, core):
        here = jnp.logical_and(zt == z, c == core)

        @pl.when(here)
        def _():
            pltpu.make_async_copy(src, dst, recv).start()

        @pl.when(jnp.logical_not(here))
        def _():
            remote(src, dst, send, recv, at(zt, x, core)).start()

    def sent_piece(src, dst, send, recv, zt, core):
        @pl.when(jnp.logical_not(jnp.logical_and(zt == z, c == core)))
        def _():
            remote(src, dst, send, recv, at(zt, x, core)).wait_send()

    cols5 = pl.ds(4 * HD, HD)

    def swap_copies():
        k_dst = 2 * z + x
        return (
            (k_in.at[:, cols5], kv5.at[k_dst, 0], 0),
            (v_in.at[:, cols5], kv5.at[k_dst, 1], 1),
            (q_in.at[:, cols5], q5, 2),
        )

    same = c == x

    def start_swap():
        for src, dst, n in swap_copies():

            @pl.when(same)
            def _():
                pltpu.make_async_copy(src, dst, f_recv.at[n]).start()

            @pl.when(jnp.logical_not(same))
            def _():
                remote(src, dst, f_send.at[n], f_recv.at[n], at(z, 1 - x, 1 - c)).start()

    def sent_swap():
        @pl.when(jnp.logical_not(same))
        def _():
            for src, dst, n in swap_copies():
                remote(src, dst, f_send.at[n], f_recv.at[n], at(z, 1 - x, 1 - c)).wait_send()

    start_swap()
    each_piece(start_piece)
    lg5[...] = jnp.zeros((8, HD), jnp.float32)

    ids = ids_ref[...]
    starts = [jnp.sum(jnp.sum(jnp.where(ids < n, 1.0, 0.0), axis=0, keepdims=True), axis=1, keepdims=True) for n in (1, 2, 3)]

    def clip_of(block):
        pos = (block * ROWS + lax.broadcasted_iota(jnp.int32, (ROWS, HD), 0)).astype(jnp.float32)
        clip = jnp.zeros((ROWS, HD), jnp.float32)
        for s in starts:
            clip = clip + jnp.where(pos >= s, 1.0, 0.0)
        return clip, lax.broadcasted_iota(jnp.int32, (ROWS, HD), 1).astype(jnp.float32)

    def fill(b, carry):
        clip, lane = clip_of(b)
        mk[b] = jnp.where(lane == clip, 0.0, jnp.where(lane < 4.0, 1.0, 0.0)).astype(jnp.bfloat16)
        return carry

    def fill_q(n, carry):
        clip, lane = clip_of(jnp.where(n == 4, kb5, 2 * (2 * n + c) + x))
        mq[n] = jnp.where(lane == clip, -APART, 0.0).astype(jnp.bfloat16)
        m_all[n] = jnp.full((ROWS, HD), -1e30, jnp.float32)
        acc_all[n] = jnp.zeros((ROWS, 2 * HD), jnp.float32)
        return carry

    def block_in(src):
        return kv.at[c, 2 * src + x]

    def to_x(src):
        return remote(block_in(src), block_in(src), x_send.at[src], x_recv.at[src], at(z, 1 - x, c))

    def to_core(b):
        return remote(kv.at[c, b], kv.at[c, b], c_send.at[b], c_recv.at[b], at(z, x, 1 - c))

    def relay(src):
        arrived(block_in(src), kv_recv.at[src])
        to_x(src).start()
        to_core(2 * src + x).start()

    def relay_x(src):
        b = 2 * src + 1 - x
        arrived(kv.at[c, b], x_recv.at[src])
        to_core(b).start()

    def c5_copy(zz):
        b = 2 * zz + c
        return remote(kv5.at[b], kv5.at[b], c5_send.at[zz], c5_recv.at[b], at(z, x, 1 - c))

    def right(s):
        b = 2 * (z - s + 1) + c
        return remote(kv5.at[b], kv5.at[b], ch_send.at[0, s - 1], chl_recv.at[s - 1], at((z + 1) % NZ, x, c))

    def left(s):
        b = 2 * (z + s - 1) + c
        return remote(kv5.at[b], kv5.at[b], ch_send.at[1, s - 1], chr_recv.at[s - 1], at((z + NZ - 1) % NZ, x, c))

    def goes_right(s):
        return jnp.logical_and(z + 1 < NZ, z - s + 1 >= 0)

    def goes_left(s):
        return jnp.logical_and(z - 1 >= 0, z + s - 1 < NZ)

    def chain(s):
        @pl.when(z - s >= 0)
        def _():
            arrived(kv5.at[2 * (z - s) + c], chl_recv.at[s - 1])
            c5_copy(z - s).start()

        if s < 3:

            @pl.when(goes_right(s + 1))
            def _():
                right(s + 1).start()

        @pl.when(z + s < NZ)
        def _():
            arrived(kv5.at[2 * (z + s) + c], chr_recv.at[s - 1])
            c5_copy(z + s).start()

        if s < 3:

            @pl.when(goes_left(s + 1))
            def _():
                left(s + 1).start()

    def offset(t):
        return ((t + 1) // 2) * (2 * (t % 2) - 1)

    def source(t):
        return (z + offset(t) + NZ) % NZ

    ones = jnp.ones((2 * ROWS, HD), jnp.bfloat16)

    def tile(n, q, zk, k_of, v_of):
        keys = [jnp.concatenate([k_of(2 * zk + l), mk[2 * zk + l]], axis=1) for l in range(2)]
        va = jnp.concatenate([jnp.concatenate([v_of(2 * zk), v_of(2 * zk + 1)], axis=0), ones], axis=1)
        for h in range(2):
            part = slice(h * HALF, (h + 1) * HALF)
            qa = jnp.concatenate([q[part, :], mq[n, part, :]], axis=1)
            scores = [
                lax.dot_general(qa, k, (((1,), (1,)), ((), ())), preferred_element_type=jnp.float32) for k in keys
            ]
            top = functools.reduce(
                jnp.maximum, [s[:, l * HD : (l + 1) * HD] for s in scores for l in range(ROWS // HD)]
            )
            m_old = m_all[n, part, :]
            m_new = jnp.maximum(m_old, jnp.max(top, axis=1, keepdims=True))
            alpha = jnp.exp2((m_old - m_new) * TO_EXP2)
            m_wide = jnp.concatenate([m_new] * (ROWS // HD), axis=1)
            p = jnp.concatenate([jnp.exp2((s - m_wide) * TO_EXP2).astype(jnp.bfloat16) for s in scores], axis=1)
            pv = jnp.dot(p, va, preferred_element_type=jnp.float32)
            acc_all[n, part, :] = acc_all[n, part, :] * jnp.concatenate([alpha, alpha], axis=1) + pv
            m_all[n, part, :] = m_new

    def finish(n):
        total = acc_all[n, :, HD:]
        out = (acc_all[n, :, :HD] / total).astype(jnp.bfloat16)
        rows = jnp.transpose(m_all[n] * SCALE + jnp.log(total))[0:1, :]
        return out, [rows[:, r * HD : (r + 1) * HD] for r in range(ROWS // HD)]

    cols_out = pl.ds(pl.multiple_of(i_head * HD, HD), HD)

    def o_dst():
        return att.at[:, cols_out]

    def o_copy(n):
        return remote(ou.at[n], o_dst(), o_send.at[n], o_recv.at[i_head], at(2 * n + c, x, g))

    def o_home(n):
        return jnp.logical_and(2 * n + c == z, c == g)

    def send_o(n):
        @pl.when(o_home(n))
        def _():
            pltpu.make_async_copy(ou.at[n], o_dst(), o_recv.at[i_head]).start()

        @pl.when(jnp.logical_not(o_home(n)))
        def _():
            o_copy(n).start()

    lax.fori_loop(0, 16, fill, 0)
    lax.fori_loop(0, 5, fill_q, 0)
    def find(b, state):
        count, found = state[0], state[1:]
        mine = plan_ref[b] == seq
        found = tuple(jnp.where(jnp.logical_and(mine, count == n), b, f) for n, f in enumerate(found))
        return (count + jnp.where(mine, 1, 0), *found)

    found = lax.fori_loop(0, 64, find, (0, 0, 0, 0, 0))[1:]

    relay(source(0))
    relay_x(source(0))

    def stage(j, carry):
        s_j = source(j)

        @pl.when(j < 7)
        def _():
            relay(source(jnp.minimum(j + 1, 7)))

        @pl.when(j == 1)
        def _():
            arrived(kv5.at[kb5, 0], f_recv.at[0])
            arrived(kv5.at[kb5, 1], f_recv.at[1])
            arrived(q5, f_recv.at[2])
            c5_copy(z).start()

            @pl.when(goes_right(1))
            def _():
                right(1).start()

            @pl.when(goes_left(1))
            def _():
                left(1).start()

        for l in range(2):
            arrived(kv.at[1 - c, 2 * s_j + l], c_recv.at[2 * s_j + l])

        @pl.when(s_j % 2 == c)
        def _():
            arrived(qu.at[s_j // 2], q_recv.at[s_j // 2])

        @pl.when(j < 7)
        def _():
            relay_x(source(jnp.minimum(j + 1, 7)))

        return carry

    lax.fori_loop(0, 8, stage, 0)

    def chunk(n, carry):
        zq = 2 * n + c

        def step(zk, inner):
            tile(n, qu.at[n], zk, lambda b: kv[0, b], lambda b: kv[1, b])
            return inner

        lax.fori_loop(jnp.maximum(zq - 3, 0), jnp.minimum(zq + 4, NZ), step, 0)
        out, rows = finish(n)
        ou[n] = out
        for r in range(4):
            lg[pl.ds(4 * n + r, 1), :] = rows[r]

        @pl.when(n > 0)
        def _():
            send_o(jnp.maximum(n - 1, 0))

        return carry

    chain(1)
    lax.fori_loop(0, 1, chunk, 0)
    chain(2)
    lax.fori_loop(1, 2, chunk, 0)
    chain(3)
    lax.fori_loop(2, 4, chunk, 0)
    send_o(3)

    def lg_copy(t):
        return remote(lg, lg_all.at[i_head, 2 * x + c], lg_send.at[t], lg_recv.at[i_head, 2 * x + c], {"seq": t, "head": 2 * xh + g})

    def lg_here(t):
        return jnp.logical_and(t == seq, c == g)

    def send_lg(t, carry):
        @pl.when(lg_here(t))
        def _():
            pltpu.make_async_copy(lg, lg_all.at[i_head, 2 * x + c], lg_recv.at[i_head, 2 * x + c]).start()

        @pl.when(jnp.logical_not(lg_here(t)))
        def _():
            lg_copy(t).start()

        return carry

    lax.fori_loop(0, 16, send_lg, 0)
    def own_there(t, carry):
        zk = z + offset(t)

        @pl.when(jnp.logical_and(zk >= 0, zk < NZ))
        def _():
            b = 2 * zk + 1 - c
            arrived(kv5.at[b], c5_recv.at[b])

        return carry

    def own(zk, carry):
        tile(4, q5, zk, lambda b: kv5[b, 0], lambda b: kv5[b, 1])
        return carry

    lax.fori_loop(0, 7, own_there, 0)
    lax.fori_loop(jnp.maximum(z - 3, 0), jnp.minimum(z + 4, NZ), own, 0)
    out, rows = finish(4)
    o5[...] = out
    for r in range(4):
        lg5[r : r + 1, :] = rows[r]

    def lg5_copy(t):
        return remote(lg5, lg5_all.at[kb5], lg5_send.at[t], lg5_recv.at[kb5], {"seq": t, "head": 2 * xh + x})

    def lg5_here(t):
        return jnp.logical_and(t == seq, c == x)

    def send_lg5(t, carry):
        @pl.when(lg5_here(t))
        def _():
            pltpu.make_async_copy(lg5, lg5_all.at[kb5], lg5_recv.at[kb5]).start()

        @pl.when(jnp.logical_not(lg5_here(t)))
        def _():
            lg5_copy(t).start()

        return carry

    o5_dst = att.at[:, cols5]

    @pl.when(same)
    def _():
        pltpu.make_async_copy(o5, o5_dst, o5_recv).start()

    @pl.when(jnp.logical_not(same))
    def _():
        remote(o5, o5_dst, o5_send, o5_recv, at(z, 1 - x, 1 - c)).start()

    lax.fori_loop(0, 16, send_lg5, 0)

    each_piece(sent_piece)
    sent_swap()
    for src in range(NZ):
        to_x(src).wait_send()
    for b in range(16):
        to_core(b).wait_send()
    for d in range(-3, 4):

        @pl.when(jnp.logical_and(z + d >= 0, z + d < NZ))
        def _():
            c5_copy(z + d).wait_send()

    for s in (1, 2, 3):

        @pl.when(goes_right(s))
        def _():
            right(s).wait_send()

        @pl.when(goes_left(s))
        def _():
            left(s).wait_send()

    for n in range(4):

        @pl.when(jnp.logical_not(o_home(n)))
        def _(n=n):
            o_copy(n).wait_send()

    def sent_lg(t, carry):
        @pl.when(jnp.logical_not(lg_here(t)))
        def _():
            lg_copy(t).wait_send()

        @pl.when(jnp.logical_not(lg5_here(t)))
        def _():
            lg5_copy(t).wait_send()

        return carry

    lax.fori_loop(0, 16, sent_lg, 0)

    @pl.when(jnp.logical_not(same))
    def _():
        remote(o5, o5_dst, o5_send, o5_recv, at(z, 1 - x, 1 - c)).wait_send()

    for i in range(4):
        for w in range(4):
            arrived(lg_all.at[i, w], lg_recv.at[i, w])
    for b in range(16):
        arrived(lg5_all.at[b], lg5_recv.at[b])
    for n, b in enumerate(found):
        w = 2 * ((b // 4) % 2) + (b // 8) % 2
        row = 4 * (b // 16) + b % 4
        for i in range(4):
            lg_out[i : i + 1, n * HD : (n + 1) * HD] = lg_all[i, w, pl.ds(row, 1), :]
        lg_out[4:5, n * HD : (n + 1) * HD] = lg5_all[b // 4, pl.ds(b % 4, 1), :]
    for i in range(4):
        arrived(att.at[:, pl.ds(i * HD, HD)], o_recv.at[i])
    arrived(o5_dst, o5_recv)


def shards(queries, keys, values, clip_ids, plan):
    vmem = pl.BlockSpec(memory_space=pltpu.VMEM)
    anywhere = pl.BlockSpec(memory_space=pl.ANY)
    bf16, f32 = jnp.bfloat16, jnp.float32
    dma = pltpu.SemaphoreType.DMA
    return pl.pallas_call(
        kernel,
        out_shape=(jax.ShapeDtypeStruct((ROWS, 5 * HD), bf16), jax.ShapeDtypeStruct((5, ROWS), f32)),
        in_specs=[anywhere, anywhere, anywhere, vmem, pl.BlockSpec(memory_space=pltpu.SMEM)],
        out_specs=(vmem, vmem),
        scratch_shapes=[
            pltpu.VMEM((2, 2 * NZ, ROWS, HD), bf16),
            pltpu.VMEM((4, ROWS, HD), bf16),
            pltpu.VMEM((4, ROWS, HD), bf16),
            pltpu.VMEM((2 * NZ, 2, ROWS, HD), bf16),
            pltpu.VMEM((ROWS, HD), bf16),
            pltpu.VMEM((ROWS, HD), bf16),
            pltpu.VMEM((2 * NZ, ROWS, HD), bf16),
            pltpu.VMEM((5, ROWS, HD), bf16),
            pltpu.VMEM((5, ROWS, HD), f32),
            pltpu.VMEM((5, ROWS, 2 * HD), f32),
            pltpu.VMEM((2 * NZ, HD), f32),
            pltpu.VMEM((8, HD), f32),
            pltpu.VMEM((4, 4, 2 * NZ, HD), f32),
            pltpu.VMEM((2 * NZ, 8, HD), f32),
            dma((4,)), dma((4,)), dma((4,)), dma((NZ,)), dma((2 * NZ,)), dma((3,)), dma((2, 3)), dma((NZ,)),
            dma((4,)), dma, dma((16,)), dma((16,)),
            dma((4,)), dma((NZ,)), dma((NZ,)), dma((2 * NZ,)), dma((3,)), dma((3,)), dma((3,)), dma((2 * NZ,)),
            dma((4,)), dma, dma((4, 4)), dma((16,)),
        ],
        compiler_params=pltpu.CompilerParams(collective_id=0, has_side_effects=True, vmem_limit_bytes=67043328),
        name="clips",
    )(queries, keys, values, clip_ids.reshape(64, HD), plan)


def solution(mesh):
    return jax.shard_map(
        shards,
        mesh=mesh,
        in_specs=(
            P(("req", "seq"), "head"),
            P(("req", "seq"), "head"),
            P(("req", "seq"), "head"),
            P("req"),
            P("req"),
        ),
        out_specs=(P(("req", "seq"), "head"), P("head", ("req", "seq"))),
        check_vma=False,
    )
```
